32 devices in a mesh: vocab: 8 (over z, y), batch: 4 (over x, core).
Axes of the slice: x: 2, y: 2, z: 4, core: 2. Of those that a mesh axis runs over, the one named last changes fastest.
Arguments:
- latent_activation: bfloat16 [3, 512, 6144], P(None, ('batch', 'vocab')), parts along dimension 1, may hold values from -6 to 6
- readout_matrix: bfloat16 [6144, 32768], P(None, 'vocab'), may hold values from -0.078125 to 0.078125
- caller_additive_shift: float32 [512, 32768], P('batch', 'vocab'), parts along dimension 0, may hold values from -4 to 600
- uniform_jitter: float32 [3, 512, 32768], P(None, 'batch', 'vocab'), parts along dimension 1, may hold values from 0.001 to 0.999
- context_word_indices: int32 [512, 256], P('batch'), parts along dimension 0, may hold values from 0 to 32767
- emitted_word_indices: int32 [512, 3], P('batch'), parts along dimension 0, may hold values from 0 to 32767
- heat_factor: float32 [512], P('batch'), parts along dimension 0, may hold values from 0.7 to 1.4
- recurrence_charge: float32 [512], P('batch'), parts along dimension 0, may hold values from 1.05 to 1.3
- appearance_charge: float32 [512], P('batch'), parts along dimension 0, may hold values from 0 to 1
- occurrence_charge: float32 [512], P('batch'), parts along dimension 0, may hold values from 0 to 1
Outputs:
- perturbed_max: float32 [3, 512], P(None, 'batch'), parts along dimension 1
- target_logprob: float32 [3, 512], P(None, 'batch'), parts along dimension 1
- last_logprobs: float32 [512, 32768], P('batch', 'vocab'), parts along dimension 0
The draws below stay inside these ranges and needn't reach their ends.
There are 4 independent parts, one for each index of `batch`. The reference program is written for one: setup_inputs(seed, part) draws one part's arguments, and reference() takes and returns one part's arrays. A program takes and returns all parts, laid end to end along the dimension named above; an argument that names none is the same for every part. Nothing has to cross between parts.
All inputs are finite; a program needn't handle non-finite values.
Results may differ from the reference program's by a relative error of at most 0.0003.
Values may be sent and summed in bfloat16 or wider, within the bound.
A program may use at most 128 MiB of HBM per device.

```python
import math
import jax
import jax.numpy as jnp
import numpy as np

D = 6144
V = 32768
BATCH_MEMBERS = 128
P_SIZE = 256
STEPS = 3


def draw_caller_additive_shift(key, part):
    base = jnp.clip(jax.random.normal(jax.random.fold_in(key, 11), (BATCH_MEMBERS, V), jnp.float32), -4.0, 4.0)
    return base


def set_ends(drawn, stream_key, least, top_value):
    dims = drawn.shape
    spot = [jax.random.randint(jax.random.fold_in(stream_key, axis), (), 0, dims[axis]) for axis in range(len(dims))]
    drawn = drawn.at[tuple(spot)].set(least)
    longest = dims.index(max(dims))
    spot[longest] = (spot[longest] + 1) % dims[longest]
    return drawn.at[tuple(spot)].set(top_value)


def shard_levels(key, shape, shards, smallest, largest):
    def one(axis_at, blocks):
        steps = jax.random.uniform(jax.random.fold_in(jax.random.fold_in(key, 6), axis_at), (blocks,), jnp.float32, smallest / len(shards), largest / len(shards))
        return jnp.repeat(jnp.exp(steps), shape[axis_at] // blocks).reshape((-1,) + (1,) * (len(shape) - axis_at - 1))

    level = one(*shards[0])
    for cut in shards[1:]:
        level = level * one(*cut)
    return level


def rank_table(amount, skew):
    loads = [(1 << 20) // math.isqrt(grade ** skew) + 1 for grade in range(1, amount + 1)]
    deviation = 1 + sum(loads) // (1 << 30)
    return np.cumsum(np.array([max(1, weight // deviation) for weight in loads]))


def skewed_ids(rng, shape, count, skew):
    listing = rank_table(count, skew)
    lot = jax.random.randint(jax.random.fold_in(rng, 1), shape, 0, int(listing[count - 1]))
    rank = jnp.searchsorted(jnp.asarray(listing, jnp.int32), lot, side="right")
    return jax.random.permutation(jax.random.fold_in(rng, 2), count)[rank].astype(jnp.int32)


def noise(rng, dims, deviation, reach, shards=(), kind=jnp.bfloat16):
    entries = jax.random.normal(rng, dims, jnp.float32) * deviation
    if len(shards) > 0:
        entries = shard_levels(rng, dims, shards, -0.22, 0.18) * entries
    return jnp.clip(entries, min=-reach, max=reach).astype(kind)


def setup_inputs(seed: int = 0, part: int = 0) -> dict:
    keys = jax.random.split(jax.random.key(seed), 11)
    part_keys = jax.random.split(jax.random.fold_in(keys[10], part), 11)
    latent_activation = noise(part_keys[0], (STEPS, BATCH_MEMBERS, D), 1.0, 6.0, ((1, 8),))
    readout_matrix = noise(keys[1], (D, V), D ** -0.5, 0.078125, ((1, 8),))
    caller_additive_shift = draw_caller_additive_shift(jax.random.fold_in(jax.random.fold_in(keys[10], part), 71), part)
    uniform_jitter = jnp.clip(0.001 + 0.998 * jax.random.uniform(part_keys[3], (STEPS, BATCH_MEMBERS, V), jnp.float32) ** shard_levels(part_keys[3], (STEPS, BATCH_MEMBERS, V), ((2, 8),), -0.2, 0.2), 0.001, 0.999)
    context_word_indices = set_ends(skewed_ids(part_keys[4], (BATCH_MEMBERS, P_SIZE), V, 2), jax.random.fold_in(part_keys[4], 3), 0, V - 1).astype(jnp.int32)
    emitted_word_indices = set_ends(skewed_ids(part_keys[5], (BATCH_MEMBERS, STEPS), V, 2), jax.random.fold_in(part_keys[5], 3), 0, V - 1).astype(jnp.int32)
    heat_factor = jnp.clip(jnp.exp(jax.random.uniform(part_keys[6], (BATCH_MEMBERS,), jnp.float32, math.log(0.7), math.log(1.4))), 0.7, 1.4)
    recurrence_charge = jnp.clip(jnp.exp(jax.random.uniform(part_keys[7], (BATCH_MEMBERS,), jnp.float32, math.log(1.05), math.log(1.3))), 1.05, 1.3)
    appearance_charge = jnp.clip(jax.random.uniform(part_keys[8], (BATCH_MEMBERS,), jnp.float32, 0.0, 1.0), 0.0, 1.0)
    occurrence_charge = jnp.clip(jax.random.uniform(part_keys[9], (BATCH_MEMBERS,), jnp.float32, 0.0, 1.0), 0.0, 1.0)
    return dict(latent_activation=latent_activation, readout_matrix=readout_matrix, caller_additive_shift=caller_additive_shift, uniform_jitter=uniform_jitter, context_word_indices=context_word_indices, emitted_word_indices=emitted_word_indices, heat_factor=heat_factor, recurrence_charge=recurrence_charge, appearance_charge=appearance_charge, occurrence_charge=occurrence_charge)


def enforce_repeat_charges(plain_energies, word_tallies, caller_additive_shift, heat_factor, recurrence_charge, appearance_charge, occurrence_charge):
    seen = word_tallies > 0
    counted = word_tallies.astype(jnp.float32)
    biased = plain_energies + caller_additive_shift
    repeat = recurrence_charge[:, None]
    cooled_energies = jnp.where(seen, jnp.where(biased > 0, biased / repeat, biased * repeat), biased)
    cooled_energies = cooled_energies - occurrence_charge[:, None] * counted - appearance_charge[:, None] * seen.astype(jnp.float32)
    return cooled_energies / heat_factor[:, None]


def reference(latent_activation, readout_matrix, caller_additive_shift, uniform_jitter, context_word_indices, emitted_word_indices, heat_factor, recurrence_charge, appearance_charge, occurrence_charge):
    batch_rows = jnp.arange(BATCH_MEMBERS, dtype=jnp.int32)
    word_tallies = jnp.zeros((BATCH_MEMBERS, V), jnp.int32).at[batch_rows[:, None], context_word_indices].add(1)
    plain_energies = jnp.dot(latent_activation.reshape(STEPS * BATCH_MEMBERS, D), readout_matrix, preferred_element_type=jnp.float32).reshape(STEPS, BATCH_MEMBERS, V)
    best_list = []
    target_list = []
    last = None
    for generation_moment in range(STEPS):
        word_energies = enforce_repeat_charges(plain_energies[generation_moment], word_tallies, caller_additive_shift, heat_factor, recurrence_charge, appearance_charge, occurrence_charge)
        gumbel = -jnp.log(-jnp.log(uniform_jitter[generation_moment]))
        best_list.append(jnp.max(word_energies + gumbel, axis=1))
        top = jnp.max(word_energies, axis=1)
        normalizer = top + jnp.log(jnp.sum(jnp.exp(word_energies - top[:, None]), axis=1))
        taken = emitted_word_indices[:, generation_moment]
        target_score = jnp.take_along_axis(word_energies, taken[:, None], axis=1)[:, 0]
        target_list.append(target_score - normalizer)
        last = word_energies - normalizer[:, None]
        word_tallies = word_tallies.at[batch_rows, taken].add(1)
    return jnp.stack(best_list), jnp.stack(target_list), last
```

```python
import functools
import math

import jax
import jax.numpy as jnp
from jax import lax
from jax.experimental import pallas as pl
from jax.experimental.pallas import tpu as pltpu
from jax.sharding import PartitionSpec as P

MESH = pl.DeviceIdType.MESH
LANES = 128
AHEAD = 2
SLOTS = 4
DOT_COLUMNS = 512
TAIL_COLUMNS = 512


def count_prompt(context_word_indices, vocab_ids):
    batch_rows, length = context_word_indices.shape
    block_size = math.gcd(length, 32)

    def add_block(turn_index, totals):
        id_block = lax.dynamic_slice_in_dim(
            context_word_indices, turn_index * block_size, block_size, 1
        )
        matches = (id_block[:, :, None] == vocab_ids[None, None, :]).astype(jnp.int32)
        return totals + jnp.sum(matches, axis=1)

    empty = jnp.zeros((batch_rows, vocab_ids.shape[0]), jnp.int32)
    return lax.fori_loop(0, length // block_size, add_block, empty)


def enforce_repeat_charges(
    plain_energies,
    word_tallies,
    caller_additive_shift,
    soften_by_heat,
    repeat,
    appearance_charge,
    occurrence_charge,
):
    seen = word_tallies > 0
    counted = word_tallies.astype(jnp.float32)
    biased = plain_energies + caller_additive_shift
    cooled_energies = jnp.where(
        seen, jnp.where(biased > 0, biased / repeat, biased * repeat), biased
    )
    cooled_energies = (
        cooled_energies - occurrence_charge * counted - appearance_charge * seen.astype(jnp.float32)
    )
    return cooled_energies / soften_by_heat


def summarize(word_energies, gumbel, target_hit):
    local_top = jnp.max(word_energies, axis=-1)
    perturbed = jnp.max(word_energies + gumbel, axis=-1)
    target_score = jnp.sum(jnp.where(target_hit, word_energies, 0.0), axis=-1)
    top, best = lax.pmax((local_top, perturbed), "vocab")
    local_sum = jnp.sum(jnp.exp(word_energies - top[..., None]), axis=-1)
    total, target_total = lax.psum((local_sum, target_score), "vocab")
    normalizer = top + jnp.log(total)
    return (best, target_total - normalizer, normalizer)


def per_device(
    latent_activation,
    readout_matrix,
    caller_additive_shift,
    uniform_jitter,
    context_word_indices,
    emitted_word_indices,
    heat_factor,
    recurrence_charge,
    appearance_charge,
    occurrence_charge,
):
    width = readout_matrix.shape[1]
    vocab_ids = lax.axis_index("vocab") * width + jnp.arange(width, dtype=jnp.int32)
    prompt_counts = count_prompt(context_word_indices, vocab_ids)
    hits = (jnp.transpose(emitted_word_indices)[:, :, None] == vocab_ids[None, None, :]).astype(
        jnp.int32
    )
    soften_by_heat = heat_factor[:, None]
    repeat = recurrence_charge[:, None]
    present = appearance_charge[:, None]
    frequent = occurrence_charge[:, None]
    gumbel_all = -jnp.log(-jnp.log(uniform_jitter))
    plain_energies = jnp.einsum(
        "sbd,dv->sbv",
        lax.all_gather(latent_activation, "vocab", axis=1, tiled=True),
        readout_matrix,
        preferred_element_type=jnp.float32,
    )
    word_tallies = prompt_counts[None] + jnp.cumsum(hits, axis=0) - hits
    word_energies = enforce_repeat_charges(
        plain_energies,
        word_tallies,
        caller_additive_shift,
        soften_by_heat,
        repeat,
        present,
        frequent,
    )
    best, target_logprob, normalizer = summarize(word_energies, gumbel_all, hits > 0)
    last = word_energies[-1] - normalizer[-1][:, None]
    return (best, target_logprob, last)


def fused_kernel(
    n,
    chunks,
    x_hbm,
    w_hbm,
    shift_hbm,
    u_hbm,
    ids_ref,
    emitted_ref,
    heat_ref,
    repeat_ref,
    appear_ref,
    occur_ref,
    scores_hbm,
    stats_out,
    xg,
    wbuf,
    acc,
    gumbel,
    shift,
    counts,
    tally,
    last,
    params,
    stats,
    exchange,
    own_sem,
    w_sem,
    in_sem,
    out_sem,
    send_sem,
    recv_sem,
    ex_send,
    ex_recv,
):
    steps, rows, _ = x_hbm.shape
    batch, width = shift_hbm.shape
    length = ids_ref.shape[1]
    depth = w_hbm.shape[0] // chunks
    high = width // LANES
    slab = steps * rows
    levels = n // 2
    me = lax.axis_index("vocab")
    z = me // 2
    y = lax.rem(me, 2)
    twin = z * 2 + (1 - y)

    u_copy = pltpu.make_async_copy(u_hbm, gumbel, in_sem.at[0])
    shift_copy = pltpu.make_async_copy(shift_hbm, shift, in_sem.at[1])

    def own_copy(chunk, t):
        return pltpu.make_async_copy(
            x_hbm.at[t, :, pl.ds(pl.multiple_of(chunk * depth, depth), depth)],
            xg.at[chunk, me, pl.ds(t * rows, rows), :],
            own_sem.at[chunk, t],
        )

    def w_copy(chunk):
        slot = lax.rem(chunk, SLOTS)
        return pltpu.make_async_copy(
            w_hbm.at[pl.ds(pl.multiple_of(chunk * depth, depth), depth), :],
            wbuf.at[slot],
            w_sem.at[slot],
        )

    def send(source, chunk, way, target):
        return pltpu.make_async_remote_copy(
            src_ref=xg.at[chunk, source],
            dst_ref=xg.at[chunk, source],
            send_sem=send_sem.at[chunk, source, way],
            recv_sem=recv_sem.at[chunk, source],
            device_id={"vocab": target},
            device_id_type=MESH,
        )

    def arrived(source, chunk):
        send(source, chunk, 0, twin).wait_recv()

    def start_own(chunk):
        for t in range(steps):
            own_copy(chunk, t).wait()
        send(me, chunk, 0, twin).start()

        @pl.when(z < levels - 1)
        def _():
            send(me, chunk, 1, me + 2).start()

        @pl.when(z > 0)
        def _():
            send(me, chunk, 2, me - 2).start()

    def relay(chunk, distance):
        @pl.when(z >= distance)
        def _():
            source = me - 2 * distance
            arrived(source, chunk)
            send(source, chunk, 0, twin).start()

            @pl.when(z < levels - 1)
            def _():
                send(source, chunk, 1, me + 2).start()

        @pl.when(z + distance < levels)
        def _():
            source = me + 2 * distance
            arrived(source, chunk)
            send(source, chunk, 0, twin).start()

            @pl.when(z > 0)
            def _():
                send(source, chunk, 2, me - 2).start()

    for chunk in range(chunks):
        for t in range(steps):
            own_copy(chunk, t).start()
    u_copy.start()
    for chunk in range(min(SLOTS, chunks)):
        w_copy(jnp.int32(chunk)).start()
    shift_copy.start()

    barrier = pltpu.get_barrier_semaphore()
    for step in range(1, n):
        pl.semaphore_signal(
            barrier,
            inc=1,
            device_id={"vocab": lax.rem(me + step, n)},
            device_id_type=MESH,
        )
    pl.semaphore_wait(barrier, n - 1)

    for chunk in range(min(AHEAD, chunks)):
        start_own(jnp.int32(chunk))

    params[...] = jnp.zeros_like(params)
    inverse_heat = 1.0 / heat_ref[...]
    params[0:1, :] = inverse_heat
    params[1:2, :] = repeat_ref[...]
    params[2:3, :] = 1.0 / repeat_ref[...]
    params[3:4, :] = appear_ref[...]
    params[4:5, :] = occur_ref[...]
    params[...] = jnp.transpose(params[...])

    def clear(j, carry):
        acc[pl.ds(pl.multiple_of(j * slab, slab), slab), :] = jnp.zeros((slab, width), jnp.float32)
        return carry

    lax.fori_loop(0, n, clear, 0)
    u_copy.wait()

    lane_rows = lax.broadcasted_iota(jnp.int32, (LANES, length), 0)
    high_rows = lax.broadcasted_iota(jnp.int32, (high, length), 0)
    batch_unroll = math.gcd(rows, 8)

    def prepare(group):
        base = pl.multiple_of(group * rows, rows)
        for t in range(steps):
            gumbel[t, pl.ds(base, rows), :] = -jnp.log(-jnp.log(gumbel[t, pl.ds(base, rows), :]))

        def count(turn, carry):
            for inner in range(batch_unroll):
                row = turn * batch_unroll + inner
                ids = ids_ref[pl.ds(base + row, 1), :]
                low = jnp.bitwise_and(ids, LANES - 1)
                top = jnp.right_shift(ids, LANES.bit_length() - 1) - me * high
                low_hot = jnp.where(lane_rows == low, 1.0, 0.0).astype(jnp.bfloat16)
                top_hot = jnp.where(high_rows == top, 1.0, 0.0).astype(jnp.bfloat16)
                tally[pl.ds(pl.multiple_of(row * high, high), high), :] = lax.dot_general(
                    top_hot,
                    low_hot,
                    (((1,), (1,)), ((), ())),
                    preferred_element_type=jnp.float32,
                )
            return carry

        lax.fori_loop(0, rows // batch_unroll, count, 0)
        for h in range(high):
            counts[pl.ds(base, rows), h * LANES : (h + 1) * LANES] = tally[
                pl.ds(h, rows, stride=high), :
            ]

    def multiply(chunk):
        w_copy(chunk).wait()
        slot = lax.rem(chunk, SLOTS)

        def tile(i, carry):
            columns = pl.ds(pl.multiple_of(i * DOT_COLUMNS, DOT_COLUMNS), DOT_COLUMNS)
            acc[:, columns] += jnp.dot(
                xg[chunk].reshape(n * slab, depth),
                wbuf[slot, :, columns],
                preferred_element_type=jnp.float32,
            )
            return carry

        lax.fori_loop(0, width // DOT_COLUMNS, tile, 0)

        @pl.when(chunk + SLOTS < chunks)
        def _():
            w_copy(chunk + SLOTS).start()

    def turn(i, carry):
        @pl.when(i + AHEAD < chunks)
        def _():
            start_own(i + AHEAD)

        for distance in range(1, levels):
            chunk = i - (distance - 1)

            @pl.when(jnp.logical_and(chunk >= 0, chunk < chunks))
            def _():
                relay(chunk, distance)

        @pl.when(i < n)
        def _():
            prepare(i)

        done = i - (levels - 1)

        @pl.when(done >= 0)
        def _():
            for level in range(levels):
                arrived(level * 2 + (1 - y), done)
            multiply(done)

        return carry

    lax.fori_loop(0, max(chunks + levels - 1, n), turn, 0)
    shift_copy.wait()

    column_ids = lax.broadcasted_iota(jnp.int32, (rows, TAIL_COLUMNS), 1) + me * width
    stat_lanes = lax.broadcasted_iota(jnp.int32, (rows, LANES), 1)

    def fold(values, combine):
        out = values[:, :LANES]
        for k in range(1, values.shape[1] // LANES):
            out = combine(out, values[:, k * LANES : (k + 1) * LANES])
        return out

    def finish(group, carry):
        base = pl.multiple_of(group * rows, rows)
        here = pl.ds(base, rows)
        inverse_heat = params[here, 0:1]
        repeat = params[here, 1:2]
        inverse_repeat = params[here, 2:3]
        appear = params[here, 3:4]
        occur = params[here, 4:5]
        taken = [emitted_ref[here, t : t + 1] for t in range(steps)]

        def score(i, state):
            columns = pl.ds(pl.multiple_of(i * TAIL_COLUMNS, TAIL_COLUMNS), TAIL_COLUMNS)
            vocab_ids = column_ids + i * TAIL_COLUMNS
            added = shift[here, columns]
            count = counts[here, columns]
            state = list(state)
            for t in range(steps):
                place = pl.ds(pl.multiple_of(group * slab + t * rows, rows), rows)
                biased = acc[place, columns] + added
                seen = count > 0
                charged = biased * jnp.where(biased > 0, inverse_repeat, repeat)
                energy = jnp.where(seen, charged - occur * count - appear, biased) * inverse_heat
                hit = vocab_ids == taken[t]
                acc[place, columns] = energy
                if t == steps - 1:
                    last[here, columns] = energy
                state[t] = jnp.maximum(state[t], fold(energy, jnp.maximum))
                state[steps + t] = jnp.maximum(
                    state[steps + t], fold(energy + gumbel[t, here, columns], jnp.maximum)
                )
                state[2 * steps + t] += fold(jnp.where(hit, energy, 0.0), jnp.add)
                count = count + jnp.where(hit, 1.0, 0.0)
            return tuple(state)

        lowest = jnp.full((rows, LANES), -jnp.inf, jnp.float32)
        zero = jnp.zeros((rows, LANES), jnp.float32)
        state = lax.fori_loop(
            0, width // TAIL_COLUMNS, score, (lowest,) * (2 * steps) + (zero,) * steps
        )
        tops = [jnp.max(state[t], axis=1, keepdims=True) for t in range(steps)]

        def sums(i, state):
            columns = pl.ds(pl.multiple_of(i * TAIL_COLUMNS, TAIL_COLUMNS), TAIL_COLUMNS)
            out = []
            for t in range(steps):
                place = pl.ds(pl.multiple_of(group * slab + t * rows, rows), rows)
                out.append(state[t] + fold(jnp.exp(acc[place, columns] - tops[t]), jnp.add))
            return tuple(out)

        totals = lax.fori_loop(0, width // TAIL_COLUMNS, sums, (zero,) * steps)
        gathered = zero
        for t in range(steps):
            best = jnp.max(state[steps + t], axis=1, keepdims=True)
            target = jnp.sum(state[2 * steps + t], axis=1, keepdims=True)
            total = jnp.sum(totals[t], axis=1, keepdims=True)
            for k, column in enumerate((tops[t], total, best, target)):
                gathered = jnp.where(stat_lanes == k * steps + t, column, gathered)
        stats[here, :] = gathered
        return carry

    lax.fori_loop(0, n, finish, 0)
    scores_copy = pltpu.make_async_copy(last, scores_hbm, out_sem.at[0])
    scores_copy.start()

    height = exchange.shape[1]
    exchange[me] = jnp.transpose(stats[...])[:height, :]

    def trade(step):
        return pltpu.make_async_remote_copy(
            src_ref=exchange.at[me],
            dst_ref=exchange.at[me],
            send_sem=ex_send.at[step],
            recv_sem=ex_recv.at[me],
            device_id={"vocab": lax.rem(me + step, n)},
            device_id_type=MESH,
        )

    for step in range(1, n):
        trade(step).start()

    def wait_sends(chunk, carry):
        send(me, chunk, 0, twin).wait_send()
        for distance in range(levels):
            for below in (True, False) if distance else (True,):
                source = me - 2 * distance if below else me + 2 * distance
                inside = z >= distance if below else z + distance < levels

                @pl.when(inside)
                def _():
                    if distance:
                        send(source, chunk, 0, twin).wait_send()
                    if below:
                        @pl.when(z < levels - 1)
                        def _():
                            send(source, chunk, 1, me + 2).wait_send()
                    if not below or distance == 0:
                        @pl.when(z > 0)
                        def _():
                            send(source, chunk, 2, me - 2).wait_send()
        return carry

    lax.fori_loop(0, chunks, wait_sends, 0)

    for step in range(1, n):
        other = lax.rem(me + step, n)
        pltpu.make_async_remote_copy(
            src_ref=exchange.at[other],
            dst_ref=exchange.at[other],
            send_sem=ex_send.at[step],
            recv_sem=ex_recv.at[other],
            device_id={"vocab": other},
            device_id_type=MESH,
        ).wait_recv()
    for step in range(1, n):
        trade(step).wait_send()

    every = exchange[...]
    tops = every[:, 0:steps, :]
    top = jnp.max(tops, axis=0)
    total = jnp.sum(every[:, steps : 2 * steps, :] * jnp.exp(tops - top[None]), axis=0)
    normalizer = top + jnp.log(total)
    stats_out[0:steps, :] = jnp.max(every[:, 2 * steps : 3 * steps, :], axis=0)
    stats_out[steps : 2 * steps, :] = (
        jnp.sum(every[:, 3 * steps : 4 * steps, :], axis=0) - normalizer
    )
    stats_out[2 * steps : 3 * steps, :] = normalizer
    scores_copy.wait()


def fused_device(n, chunks, *args):
    (x, w, shift, u, ids, emitted, heat, repeat, appear, occur) = args
    steps, rows, model = x.shape
    batch, width = shift.shape
    depth = model // chunks
    high = width // LANES
    height = -(-4 * steps // 8) * 8
    anywhere = pl.BlockSpec(memory_space=pl.ANY)
    inside = pl.BlockSpec(memory_space=pltpu.VMEM)
    dma = pltpu.SemaphoreType.DMA
    scores, stats = pl.pallas_call(
        functools.partial(fused_kernel, n, chunks),
        out_shape=(
            jax.ShapeDtypeStruct((batch, width), jnp.float32),
            jax.ShapeDtypeStruct((3 * steps, batch), jnp.float32),
        ),
        in_specs=[anywhere] * 4 + [inside] * 6,
        out_specs=(anywhere, inside),
        scratch_shapes=[
            pltpu.VMEM((chunks, n, steps * rows, depth), x.dtype),
            pltpu.VMEM((SLOTS, depth, width), w.dtype),
            pltpu.VMEM((steps * batch, width), jnp.float32),
            pltpu.VMEM((steps, batch, width), jnp.float32),
            pltpu.VMEM((batch, width), jnp.float32),
            pltpu.VMEM((batch, width), jnp.float32),
            pltpu.VMEM((rows * high, LANES), jnp.float32),
            pltpu.VMEM((batch, width), jnp.float32),
            pltpu.VMEM((LANES, LANES), jnp.float32),
            pltpu.VMEM((batch, LANES), jnp.float32),
            pltpu.VMEM((n, height, batch), jnp.float32),
            dma((chunks, steps)),
            dma((SLOTS,)),
            dma((2,)),
            dma((1,)),
            dma((chunks, n, 3)),
            dma((chunks, n)),
            dma((n,)),
            dma((n,)),
        ],
        compiler_params=pltpu.CompilerParams(
            collective_id=0, has_side_effects=True, vmem_limit_bytes=60 * 1024 * 1024
        ),
    )(
        x,
        w,
        shift,
        u,
        ids,
        emitted,
        heat[None],
        repeat[None],
        appear[None],
        occur[None],
    )
    best = stats[:steps]
    target_logprob = stats[steps : 2 * steps]
    return best, target_logprob, scores - stats[3 * steps - 1][:, None]


def per_device_any(n, *args):
    x, w, shift = args[:3]
    steps, rows, model = x.shape
    batch, width = shift.shape
    chunks = 12
    fits = (
        n % 2 == 0
        and n > 2
        and rows % 16 == 0
        and batch == LANES
        and rows * n == batch
        and width % max(DOT_COLUMNS, TAIL_COLUMNS) == 0
        and (width // LANES) % 8 == 0
        and model % (chunks * LANES) == 0
        and args[4].shape[1] % LANES == 0
        and 4 * steps <= LANES
    )
    if fits:
        return fused_device(n, chunks, *args)
    return per_device(*args)


def solution(mesh):
    in_specs = (
        P(None, ("batch", "vocab"), None),
        P(None, "vocab"),
        P("batch", "vocab"),
        P(None, "batch", "vocab"),
        P("batch", None),
        P("batch", None),
        P("batch"),
        P("batch"),
        P("batch"),
        P("batch"),
    )
    out_specs = (P(None, "batch"), P(None, "batch"), P("batch", "vocab"))
    return jax.shard_map(
        functools.partial(per_device_any, mesh.shape["vocab"]),
        mesh=mesh, in_specs=in_specs, out_specs=out_specs, check_vma=False
    )
```

```python
import functools
import math

import jax
import jax.numpy as jnp
from jax import lax
from jax.experimental import pallas as pl
from jax.experimental.pallas import tpu as pltpu
from jax.sharding import PartitionSpec as P

MESH = pl.DeviceIdType.MESH
LANES = 128
AHEAD = 3
SLOTS = 3
DOT_COLUMNS = 2048
TAIL_COLUMNS = 1024


def count_prompt(context_word_indices, vocab_ids):
    batch_rows, length = context_word_indices.shape
    block_size = math.gcd(length, 32)

    def add_block(turn_index, totals):
        id_block = lax.dynamic_slice_in_dim(
            context_word_indices, turn_index * block_size, block_size, 1
        )
        matches = (id_block[:, :, None] == vocab_ids[None, None, :]).astype(jnp.int32)
        return totals + jnp.sum(matches, axis=1)

    empty = jnp.zeros((batch_rows, vocab_ids.shape[0]), jnp.int32)
    return lax.fori_loop(0, length // block_size, add_block, empty)


def enforce_repeat_charges(
    plain_energies,
    word_tallies,
    caller_additive_shift,
    soften_by_heat,
    repeat,
    appearance_charge,
    occurrence_charge,
):
    seen = word_tallies > 0
    counted = word_tallies.astype(jnp.float32)
    biased = plain_energies + caller_additive_shift
    cooled_energies = jnp.where(
        seen, jnp.where(biased > 0, biased / repeat, biased * repeat), biased
    )
    cooled_energies = (
        cooled_energies - occurrence_charge * counted - appearance_charge * seen.astype(jnp.float32)
    )
    return cooled_energies / soften_by_heat


def summarize(word_energies, gumbel, target_hit):
    local_top = jnp.max(word_energies, axis=-1)
    perturbed = jnp.max(word_energies + gumbel, axis=-1)
    target_score = jnp.sum(jnp.where(target_hit, word_energies, 0.0), axis=-1)
    top, best = lax.pmax((local_top, perturbed), "vocab")
    local_sum = jnp.sum(jnp.exp(word_energies - top[..., None]), axis=-1)
    total, target_total = lax.psum((local_sum, target_score), "vocab")
    normalizer = top + jnp.log(total)
    return (best, target_total - normalizer, normalizer)


def per_device(
    latent_activation,
    readout_matrix,
    caller_additive_shift,
    uniform_jitter,
    context_word_indices,
    emitted_word_indices,
    heat_factor,
    recurrence_charge,
    appearance_charge,
    occurrence_charge,
):
    width = readout_matrix.shape[1]
    vocab_ids = lax.axis_index("vocab") * width + jnp.arange(width, dtype=jnp.int32)
    prompt_counts = count_prompt(context_word_indices, vocab_ids)
    hits = (jnp.transpose(emitted_word_indices)[:, :, None] == vocab_ids[None, None, :]).astype(
        jnp.int32
    )
    soften_by_heat = heat_factor[:, None]
    repeat = recurrence_charge[:, None]
    present = appearance_charge[:, None]
    frequent = occurrence_charge[:, None]
    gumbel_all = -jnp.log(-jnp.log(uniform_jitter))
    plain_energies = jnp.einsum(
        "sbd,dv->sbv",
        lax.all_gather(latent_activation, "vocab", axis=1, tiled=True),
        readout_matrix,
        preferred_element_type=jnp.float32,
    )
    word_tallies = prompt_counts[None] + jnp.cumsum(hits, axis=0) - hits
    word_energies = enforce_repeat_charges(
        plain_energies,
        word_tallies,
        caller_additive_shift,
        soften_by_heat,
        repeat,
        present,
        frequent,
    )
    best, target_logprob, normalizer = summarize(word_energies, gumbel_all, hits > 0)
    last = word_energies[-1] - normalizer[-1][:, None]
    return (best, target_logprob, last)


def fused_kernel(
    n,
    chunks,
    x_hbm,
    w_hbm,
    shift_hbm,
    u_hbm,
    ids_ref,
    emitted_ref,
    heat_ref,
    repeat_ref,
    appear_ref,
    occur_ref,
    scores_hbm,
    stats_out,
    xg,
    wbuf,
    acc,
    gumbel,
    strong,
    weak,
    charge,
    tally,
    energies,
    params,
    stats,
    exchange,
    own_sem,
    w_sem,
    in_sem,
    out_sem,
    send_sem,
    recv_sem,
    ex_send,
    ex_recv,
):
    steps, rows, _ = x_hbm.shape
    batch, width = shift_hbm.shape
    length = ids_ref.shape[1]
    depth = w_hbm.shape[0] // chunks
    high = width // LANES
    slab = steps * rows
    levels = n // 2
    me = lax.axis_index("vocab")
    z = me // 2
    y = lax.rem(me, 2)
    twin = z * 2 + (1 - y)

    u_copy = pltpu.make_async_copy(u_hbm, gumbel, in_sem.at[0])

    def shift_copy(group, t):
        return pltpu.make_async_copy(
            shift_hbm.at[pl.ds(group * rows, rows), :],
            acc.at[pl.ds(group * slab + t * rows, rows), :],
            in_sem.at[1 + group * steps + t],
        )

    def own_copy(chunk, t):
        return pltpu.make_async_copy(
            x_hbm.at[t, :, pl.ds(pl.multiple_of(chunk * depth, depth), depth)],
            xg.at[chunk, me, pl.ds(t * rows, rows), :],
            own_sem.at[chunk, t],
        )

    def w_copy(chunk):
        slot = lax.rem(chunk, SLOTS)
        return pltpu.make_async_copy(
            w_hbm.at[pl.ds(pl.multiple_of(chunk * depth, depth), depth), :],
            wbuf.at[slot],
            w_sem.at[slot],
        )

    def send(source, chunk, way, target):
        return pltpu.make_async_remote_copy(
            src_ref=xg.at[chunk, source],
            dst_ref=xg.at[chunk, source],
            send_sem=send_sem.at[chunk, source, way],
            recv_sem=recv_sem.at[chunk, source],
            device_id={"vocab": target},
            device_id_type=MESH,
        )

    def arrived(source, chunk):
        send(source, chunk, 0, twin).wait_recv()

    def start_own(chunk):
        for t in range(steps):
            own_copy(chunk, t).wait()
        send(me, chunk, 0, twin).start()

        pass_along(me, chunk)

    def across_first(chunk):
        return lax.rem(chunk, 6) == 2

    def pass_along(source, chunk):
        @pl.when(z < levels - 1)
        def _():
            send(source, chunk, 1, me + 2).start()

        @pl.when(z > 0)
        def _():
            send(source, chunk, 2, me - 2).start()

    def relay_twin(chunk, distance):
        if distance == 0:
            arrived(twin, chunk)
            pass_along(twin, chunk)
            return

        @pl.when(z >= distance)
        def _():
            source = twin - 2 * distance
            arrived(source, chunk)

            @pl.when(z < levels - 1)
            def _():
                send(source, chunk, 1, me + 2).start()

        @pl.when(z + distance < levels)
        def _():
            source = twin + 2 * distance
            arrived(source, chunk)

            @pl.when(z > 0)
            def _():
                send(source, chunk, 2, me - 2).start()

    def relay(chunk, distance):
        @pl.when(z >= distance)
        def _():
            source = me - 2 * distance
            arrived(source, chunk)

            @pl.when(jnp.logical_not(across_first(chunk)))
            def _():
                send(source, chunk, 0, twin).start()

            @pl.when(z < levels - 1)
            def _():
                send(source, chunk, 1, me + 2).start()

        @pl.when(z + distance < levels)
        def _():
            source = me + 2 * distance
            arrived(source, chunk)

            @pl.when(jnp.logical_not(across_first(chunk)))
            def _():
                send(source, chunk, 0, twin).start()

            @pl.when(z > 0)
            def _():
                send(source, chunk, 2, me - 2).start()

    for chunk in range(chunks):
        for t in range(steps):
            own_copy(chunk, t).start()
    u_copy.start()
    for chunk in range(min(SLOTS, chunks)):
        w_copy(jnp.int32(chunk)).start()
    for group in range(n):
        for t in range(steps):
            shift_copy(group, t).start()

    barrier = pltpu.get_barrier_semaphore()
    for step in range(1, n):
        pl.semaphore_signal(
            barrier,
            inc=1,
            device_id={"vocab": lax.rem(me + step, n)},
            device_id_type=MESH,
        )
    pl.semaphore_wait(barrier, n - 1)

    for chunk in range(min(AHEAD, chunks)):
        start_own(jnp.int32(chunk))

    params[...] = jnp.zeros_like(params)
    inverse_heat = 1.0 / heat_ref[...]
    params[0:1, :] = inverse_heat
    params[1:2, :] = repeat_ref[...] * inverse_heat
    params[2:3, :] = inverse_heat / repeat_ref[...]
    params[3:4, :] = appear_ref[...] * inverse_heat
    params[4:5, :] = occur_ref[...] * inverse_heat
    params[5 : 5 + steps, :] = emitted_ref[...].astype(jnp.float32)
    params[...] = jnp.transpose(params[...])

    u_copy.wait()
    for group in range(n):
        for t in range(steps):
            shift_copy(group, t).wait()

    lane_rows = lax.broadcasted_iota(jnp.int32, (LANES, length), 0)
    high_rows = lax.broadcasted_iota(jnp.int32, (high, length), 0)
    batch_unroll = math.gcd(rows, 8)
    lane_ids = lax.broadcasted_iota(jnp.int32, (rows, LANES), 1)

    def prepare(group):
        base = pl.multiple_of(group * rows, rows)
        for t in range(steps):
            gumbel[t, pl.ds(base, rows), :] = -jnp.log(-jnp.log(gumbel[t, pl.ds(base, rows), :]))

        def count(turn, carry):
            for inner in range(batch_unroll):
                row = turn * batch_unroll + inner
                ids = ids_ref[pl.ds(base + row, 1), :]
                low = jnp.bitwise_and(ids, LANES - 1)
                top = jnp.right_shift(ids, LANES.bit_length() - 1) - me * high
                low_hot = jnp.where(lane_rows == low, 1.0, 0.0).astype(jnp.bfloat16)
                top_hot = jnp.where(high_rows == top, 1.0, 0.0).astype(jnp.bfloat16)
                tally[pl.ds(pl.multiple_of(row * high, high), high), :] = lax.dot_general(
                    top_hot,
                    low_hot,
                    (((1,), (1,)), ((), ())),
                    preferred_element_type=jnp.float32,
                )
            return carry

        lax.fori_loop(0, rows // batch_unroll, count, 0)
        here = pl.ds(base, rows)
        plain, repeat, inverse_repeat, appear, occur = (
            jnp.broadcast_to(params[here, k : k + 1], (rows, LANES)) for k in range(5)
        )
        taken = [
            jnp.broadcast_to(params[here, 5 + t : 6 + t], (rows, LANES)).astype(jnp.int32)
            for t in range(steps)
        ]
        for h in range(high):
            count = tally[pl.ds(h, rows, stride=high), :]
            columns = slice(h * LANES, (h + 1) * LANES)
            for t in range(steps):
                place = pl.ds(pl.multiple_of(group * slab + t * rows, rows), rows)
                seen = count > 0
                strong[place, columns] = jnp.where(seen, repeat, plain)
                weak[place, columns] = jnp.where(seen, inverse_repeat, plain)
                charge[place, columns] = jnp.where(seen, occur * count + appear, 0.0)
                hit = lane_ids + (me * width + h * LANES) == taken[t]
                count = count + jnp.where(hit, 1.0, 0.0)

    def multiply(chunk):
        w_copy(chunk).wait()
        slot = lax.rem(chunk, SLOTS)

        def tile(i, carry):
            columns = pl.ds(pl.multiple_of(i * DOT_COLUMNS, DOT_COLUMNS), DOT_COLUMNS)
            acc[:, columns] += jnp.dot(
                xg[chunk].reshape(n * slab, depth),
                wbuf[slot, :, columns],
                preferred_element_type=jnp.float32,
            )
            return carry

        lax.fori_loop(0, width // DOT_COLUMNS, tile, 0)

        @pl.when(chunk + SLOTS < chunks)
        def _():
            w_copy(chunk + SLOTS).start()

    def turn(i, carry):
        for distance in reversed(range(1, levels)):
            chunk = i - (distance - 1)

            @pl.when(jnp.logical_and(chunk >= 0, chunk < chunks))
            def _():
                relay(chunk, distance)

        for distance in reversed(range(levels - 1)):
            chunk = i - distance

            @pl.when(
                jnp.logical_and(
                    jnp.logical_and(chunk >= 0, chunk < chunks), across_first(chunk)
                )
            )
            def _():
                relay_twin(chunk, distance)

        @pl.when(i + AHEAD < chunks)
        def _():
            start_own(i + AHEAD)

        @pl.when(i < n)
        def _():
            prepare(i)

        done = i - (levels - 1)

        @pl.when(done >= 0)
        def _():
            for level in range(levels):
                relayed = jnp.abs(z - level) < levels - 1

                @pl.when(jnp.logical_not(jnp.logical_and(across_first(done), relayed)))
                def _():
                    arrived(level * 2 + (1 - y), done)

            multiply(done)

        return carry

    lax.fori_loop(0, max(chunks + levels - 1, n), turn, 0)

    column_ids = lane_ids + me * width
    stat_lanes = lane_ids

    def scores_copy(group):
        top_row = pl.multiple_of(group * slab + (steps - 1) * rows, rows)
        return pltpu.make_async_copy(
            energies.at[pl.ds(top_row, rows), :],
            scores_hbm.at[pl.ds(pl.multiple_of(group * rows, rows), rows), :],
            out_sem.at[group],
        )

    def finish(group, carry):
        base = pl.multiple_of(group * rows, rows)
        here = pl.ds(base, rows)
        taken = [
            jnp.broadcast_to(params[here, 5 + t : 6 + t], (rows, LANES)).astype(jnp.int32)
            for t in range(steps)
        ]

        def score(i, state):
            state = list(state)
            for k in range(TAIL_COLUMNS // LANES):
                start = pl.multiple_of(i * TAIL_COLUMNS + k * LANES, LANES)
                columns = pl.ds(start, LANES)
                vocab_ids = column_ids + start
                for t in range(steps):
                    place = pl.ds(pl.multiple_of(group * slab + t * rows, rows), rows)
                    biased = acc[place, columns]
                    energy = (
                        jnp.minimum(biased * strong[place, columns], biased * weak[place, columns])
                        - charge[place, columns]
                    )
                    energies[place, columns] = energy
                    state[t] = jnp.maximum(state[t], energy)
                    state[steps + t] = jnp.maximum(
                        state[steps + t], energy + gumbel[t, here, columns]
                    )
                    state[2 * steps + t] += jnp.where(vocab_ids == taken[t], energy, 0.0)
            return tuple(state)

        lowest = jnp.full((rows, LANES), -jnp.inf, jnp.float32)
        zero = jnp.zeros((rows, LANES), jnp.float32)
        state = lax.fori_loop(
            0, width // TAIL_COLUMNS, score, (lowest,) * (2 * steps) + (zero,) * steps
        )
        scores_copy(group).start()
        tops = [jnp.max(state[t], axis=1, keepdims=True) for t in range(steps)]

        wide_tops = [jnp.broadcast_to(top, (rows, LANES)) for top in tops]

        def sums(i, state):
            state = list(state)
            for k in range(TAIL_COLUMNS // LANES):
                start = pl.multiple_of(i * TAIL_COLUMNS + k * LANES, LANES)
                for t in range(steps):
                    place = pl.ds(pl.multiple_of(group * slab + t * rows, rows), rows)
                    state[t] += jnp.exp(energies[place, pl.ds(start, LANES)] - wide_tops[t])
            return tuple(state)

        totals = lax.fori_loop(0, width // TAIL_COLUMNS, sums, (zero,) * steps)
        gathered = zero
        for t in range(steps):
            best = jnp.max(state[steps + t], axis=1, keepdims=True)
            target = jnp.sum(state[2 * steps + t], axis=1, keepdims=True)
            total = jnp.sum(totals[t], axis=1, keepdims=True)
            for k, column in enumerate((tops[t], total, best, target)):
                gathered = jnp.where(stat_lanes == k * steps + t, column, gathered)
        stats[here, :] = gathered
        return carry

    lax.fori_loop(0, n, finish, 0)

    height = exchange.shape[1]
    exchange[me] = jnp.transpose(stats[...])[:height, :]

    def trade(step):
        return pltpu.make_async_remote_copy(
            src_ref=exchange.at[me],
            dst_ref=exchange.at[me],
            send_sem=ex_send.at[step],
            recv_sem=ex_recv.at[me],
            device_id={"vocab": lax.rem(me + step, n)},
            device_id_type=MESH,
        )

    for step in range(1, n):
        trade(step).start()

    def wait_sends(chunk, carry):
        across = across_first(chunk)
        send(me, chunk, 0, twin).wait_send()
        for level in range(levels):

            @pl.when(jnp.logical_and(level != z, jnp.logical_not(across)))
            def _():
                send(level * 2 + y, chunk, 0, twin).wait_send()

            @pl.when(jnp.logical_and(level <= z, z < levels - 1))
            def _():
                send(level * 2 + y, chunk, 1, me + 2).wait_send()

                @pl.when(across)
                def _():
                    send(level * 2 + 1 - y, chunk, 1, me + 2).wait_send()

            @pl.when(jnp.logical_and(level >= z, z > 0))
            def _():
                send(level * 2 + y, chunk, 2, me - 2).wait_send()

                @pl.when(across)
                def _():
                    send(level * 2 + 1 - y, chunk, 2, me - 2).wait_send()

        return carry

    lax.fori_loop(0, chunks, wait_sends, 0)

    for step in range(1, n):
        other = lax.rem(me + step, n)
        pltpu.make_async_remote_copy(
            src_ref=exchange.at[other],
            dst_ref=exchange.at[other],
            send_sem=ex_send.at[step],
            recv_sem=ex_recv.at[other],
            device_id={"vocab": other},
            device_id_type=MESH,
        ).wait_recv()
    for step in range(1, n):
        trade(step).wait_send()

    every = exchange[...]
    tops = every[:, 0:steps, :]
    top = jnp.max(tops, axis=0)
    total = jnp.sum(every[:, steps : 2 * steps, :] * jnp.exp(tops - top[None]), axis=0)
    normalizer = top + jnp.log(total)
    stats_out[0:steps, :] = jnp.max(every[:, 2 * steps : 3 * steps, :], axis=0)
    stats_out[steps : 2 * steps, :] = (
        jnp.sum(every[:, 3 * steps : 4 * steps, :], axis=0) - normalizer
    )
    stats_out[2 * steps : 3 * steps, :] = normalizer
    for group in range(n):
        scores_copy(jnp.int32(group)).wait()


def fused_device(n, chunks, *args):
    (x, w, shift, u, ids, emitted, heat, repeat, appear, occur) = args
    steps, rows, model = x.shape
    batch, width = shift.shape
    depth = model // chunks
    high = width // LANES
    height = -(-4 * steps // 8) * 8
    anywhere = pl.BlockSpec(memory_space=pl.ANY)
    inside = pl.BlockSpec(memory_space=pltpu.VMEM)
    dma = pltpu.SemaphoreType.DMA
    scores, stats = pl.pallas_call(
        functools.partial(fused_kernel, n, chunks),
        out_shape=(
            jax.ShapeDtypeStruct((batch, width), jnp.float32),
            jax.ShapeDtypeStruct((3 * steps, batch), jnp.float32),
        ),
        in_specs=[anywhere] * 4 + [inside] * 6,
        out_specs=(anywhere, inside),
        scratch_shapes=[
            pltpu.VMEM((chunks, n, steps * rows, depth), x.dtype),
            pltpu.VMEM((SLOTS, depth, width), w.dtype),
            pltpu.VMEM((steps * batch, width), jnp.float32),
            pltpu.VMEM((steps, batch, width), jnp.float32),
            pltpu.VMEM((steps * batch, width), jnp.float32),
            pltpu.VMEM((steps * batch, width), jnp.float32),
            pltpu.VMEM((steps * batch, width), jnp.float32),
            pltpu.VMEM((rows * high, LANES), jnp.float32),
            pltpu.VMEM((steps * batch, width), jnp.float32),
            pltpu.VMEM((LANES, LANES), jnp.float32),
            pltpu.VMEM((batch, LANES), jnp.float32),
            pltpu.VMEM((n, height, batch), jnp.float32),
            dma((chunks, steps)),
            dma((SLOTS,)),
            dma((1 + n * steps,)),
            dma((n,)),
            dma((chunks, n, 3)),
            dma((chunks, n)),
            dma((n,)),
            dma((n,)),
        ],
        compiler_params=pltpu.CompilerParams(
            collective_id=0, has_side_effects=True, vmem_limit_bytes=60 * 1024 * 1024
        ),
    )(
        x,
        w,
        shift,
        u,
        ids,
        jnp.transpose(emitted),
        heat[None],
        repeat[None],
        appear[None],
        occur[None],
    )
    best = stats[:steps]
    target_logprob = stats[steps : 2 * steps]
    return best, target_logprob, scores - stats[3 * steps - 1][:, None]


def per_device_any(n, *args):
    x, w, shift = args[:3]
    steps, rows, model = x.shape
    batch, width = shift.shape
    chunks = 12
    fits = (
        n % 2 == 0
        and n > 2
        and rows % 16 == 0
        and batch == LANES
        and rows * n == batch
        and width % max(DOT_COLUMNS, TAIL_COLUMNS) == 0
        and (width // LANES) % 8 == 0
        and model % (chunks * LANES) == 0
        and args[4].shape[1] % LANES == 0
        and 4 * steps <= LANES
    )
    if fits:
        return fused_device(n, chunks, *args)
    return per_device(*args)


def solution(mesh):
    in_specs = (
        P(None, ("batch", "vocab"), None),
        P(None, "vocab"),
        P("batch", "vocab"),
        P(None, "batch", "vocab"),
        P("batch", None),
        P("batch", None),
        P("batch"),
        P("batch"),
        P("batch"),
        P("batch"),
    )
    out_specs = (P(None, "batch"), P(None, "batch"), P("batch", "vocab"))
    return jax.shard_map(
        functools.partial(per_device_any, mesh.shape["vocab"]),
        mesh=mesh, in_specs=in_specs, out_specs=out_specs, check_vma=False
    )
```

```python
import functools
import math

import jax
import jax.numpy as jnp
from jax import lax
from jax.experimental import pallas as pl
from jax.experimental.pallas import tpu as pltpu
from jax.sharding import PartitionSpec as P

MESH = pl.DeviceIdType.MESH
LANES = 128
AHEAD = 4
SLOTS = 3
DOT_COLUMNS = 2048
TAIL_COLUMNS = 1024


def count_prompt(context_word_indices, vocab_ids):
    batch_rows, length = context_word_indices.shape
    block_size = math.gcd(length, 32)

    def add_block(turn_index, totals):
        id_block = lax.dynamic_slice_in_dim(
            context_word_indices, turn_index * block_size, block_size, 1
        )
        matches = (id_block[:, :, None] == vocab_ids[None, None, :]).astype(jnp.int32)
        return totals + jnp.sum(matches, axis=1)

    empty = jnp.zeros((batch_rows, vocab_ids.shape[0]), jnp.int32)
    return lax.fori_loop(0, length // block_size, add_block, empty)


def enforce_repeat_charges(
    plain_energies,
    word_tallies,
    caller_additive_shift,
    soften_by_heat,
    repeat,
    appearance_charge,
    occurrence_charge,
):
    seen = word_tallies > 0
    counted = word_tallies.astype(jnp.float32)
    biased = plain_energies + caller_additive_shift
    cooled_energies = jnp.where(
        seen, jnp.where(biased > 0, biased / repeat, biased * repeat), biased
    )
    cooled_energies = (
        cooled_energies - occurrence_charge * counted - appearance_charge * seen.astype(jnp.float32)
    )
    return cooled_energies / soften_by_heat


def summarize(word_energies, gumbel, target_hit):
    local_top = jnp.max(word_energies, axis=-1)
    perturbed = jnp.max(word_energies + gumbel, axis=-1)
    target_score = jnp.sum(jnp.where(target_hit, word_energies, 0.0), axis=-1)
    top, best = lax.pmax((local_top, perturbed), "vocab")
    local_sum = jnp.sum(jnp.exp(word_energies - top[..., None]), axis=-1)
    total, target_total = lax.psum((local_sum, target_score), "vocab")
    normalizer = top + jnp.log(total)
    return (best, target_total - normalizer, normalizer)


def per_device(
    latent_activation,
    readout_matrix,
    caller_additive_shift,
    uniform_jitter,
    context_word_indices,
    emitted_word_indices,
    heat_factor,
    recurrence_charge,
    appearance_charge,
    occurrence_charge,
):
    width = readout_matrix.shape[1]
    vocab_ids = lax.axis_index("vocab") * width + jnp.arange(width, dtype=jnp.int32)
    prompt_counts = count_prompt(context_word_indices, vocab_ids)
    hits = (jnp.transpose(emitted_word_indices)[:, :, None] == vocab_ids[None, None, :]).astype(
        jnp.int32
    )
    soften_by_heat = heat_factor[:, None]
    repeat = recurrence_charge[:, None]
    present = appearance_charge[:, None]
    frequent = occurrence_charge[:, None]
    gumbel_all = -jnp.log(-jnp.log(uniform_jitter))
    plain_energies = jnp.einsum(
        "sbd,dv->sbv",
        lax.all_gather(latent_activation, "vocab", axis=1, tiled=True),
        readout_matrix,
        preferred_element_type=jnp.float32,
    )
    word_tallies = prompt_counts[None] + jnp.cumsum(hits, axis=0) - hits
    word_energies = enforce_repeat_charges(
        plain_energies,
        word_tallies,
        caller_additive_shift,
        soften_by_heat,
        repeat,
        present,
        frequent,
    )
    best, target_logprob, normalizer = summarize(word_energies, gumbel_all, hits > 0)
    last = word_energies[-1] - normalizer[-1][:, None]
    return (best, target_logprob, last)


def fused_kernel(
    n,
    chunks,
    x_hbm,
    w_hbm,
    shift_hbm,
    u_hbm,
    ids_ref,
    emitted_ref,
    heat_ref,
    repeat_ref,
    appear_ref,
    occur_ref,
    scores_hbm,
    stats_out,
    xg,
    wbuf,
    acc,
    gumbel,
    strong,
    weak,
    charge,
    tally,
    energies,
    params,
    stats,
    exchange,
    own_sem,
    w_sem,
    in_sem,
    out_sem,
    send_sem,
    recv_sem,
    ex_send,
    ex_recv,
):
    steps, rows, _ = x_hbm.shape
    batch, width = shift_hbm.shape
    length = ids_ref.shape[1]
    depth = w_hbm.shape[0] // chunks
    high = width // LANES
    slab = steps * rows
    levels = n // 2
    me = lax.axis_index("vocab")
    z = me // 2
    y = lax.rem(me, 2)
    twin = z * 2 + (1 - y)

    u_copy = pltpu.make_async_copy(u_hbm, gumbel, in_sem.at[0])

    def shift_copy(group, t):
        return pltpu.make_async_copy(
            shift_hbm.at[pl.ds(group * rows, rows), :],
            acc.at[pl.ds(group * slab + t * rows, rows), :],
            in_sem.at[1 + group * steps + t],
        )

    def own_copy(chunk, t):
        return pltpu.make_async_copy(
            x_hbm.at[t, :, pl.ds(pl.multiple_of(chunk * depth, depth), depth)],
            xg.at[chunk, me, pl.ds(t * rows, rows), :],
            own_sem.at[chunk, t],
        )

    def w_copy(chunk):
        slot = lax.rem(chunk, SLOTS)
        return pltpu.make_async_copy(
            w_hbm.at[pl.ds(pl.multiple_of(chunk * depth, depth), depth), :],
            wbuf.at[slot],
            w_sem.at[slot],
        )

    def send(source, chunk, way, target):
        return pltpu.make_async_remote_copy(
            src_ref=xg.at[chunk, source],
            dst_ref=xg.at[chunk, source],
            send_sem=send_sem.at[chunk, source, way],
            recv_sem=recv_sem.at[chunk, source],
            device_id={"vocab": target},
            device_id_type=MESH,
        )

    def arrived(source, chunk):
        send(source, chunk, 0, twin).wait_recv()

    def start_own(chunk):
        for t in range(steps):
            own_copy(chunk, t).wait()
        send(me, chunk, 0, twin).start()

        pass_along(me, chunk)

    def across_first(chunk):
        return lax.rem(chunk, 6) == 2

    def pass_along(source, chunk):
        @pl.when(z < levels - 1)
        def _():
            send(source, chunk, 1, me + 2).start()

        @pl.when(z > 0)
        def _():
            send(source, chunk, 2, me - 2).start()

    def relay_twin(chunk, distance):
        if distance == 0:
            arrived(twin, chunk)
            pass_along(twin, chunk)
            return

        @pl.when(z >= distance)
        def _():
            source = twin - 2 * distance
            arrived(source, chunk)

            @pl.when(z < levels - 1)
            def _():
                send(source, chunk, 1, me + 2).start()

        @pl.when(z + distance < levels)
        def _():
            source = twin + 2 * distance
            arrived(source, chunk)

            @pl.when(z > 0)
            def _():
                send(source, chunk, 2, me - 2).start()

    def relay(chunk, distance):
        @pl.when(z >= distance)
        def _():
            source = me - 2 * distance
            arrived(source, chunk)

            @pl.when(jnp.logical_not(across_first(chunk)))
            def _():
                send(source, chunk, 0, twin).start()

            @pl.when(z < levels - 1)
            def _():
                send(source, chunk, 1, me + 2).start()

        @pl.when(z + distance < levels)
        def _():
            source = me + 2 * distance
            arrived(source, chunk)

            @pl.when(jnp.logical_not(across_first(chunk)))
            def _():
                send(source, chunk, 0, twin).start()

            @pl.when(z > 0)
            def _():
                send(source, chunk, 2, me - 2).start()

    for chunk in range(chunks):
        for t in range(steps):
            own_copy(chunk, t).start()
    u_copy.start()
    for chunk in range(min(SLOTS, chunks)):
        w_copy(jnp.int32(chunk)).start()
    for group in range(n):
        for t in range(steps):
            shift_copy(group, t).start()

    barrier = pltpu.get_barrier_semaphore()
    for step in range(1, n):
        pl.semaphore_signal(
            barrier,
            inc=1,
            device_id={"vocab": lax.rem(me + step, n)},
            device_id_type=MESH,
        )
    pl.semaphore_wait(barrier, n - 1)

    for chunk in range(min(AHEAD, chunks)):
        start_own(jnp.int32(chunk))

    params[...] = jnp.zeros_like(params)
    inverse_heat = 1.0 / heat_ref[...]
    params[0:1, :] = inverse_heat
    params[1:2, :] = repeat_ref[...] * inverse_heat
    params[2:3, :] = inverse_heat / repeat_ref[...]
    params[3:4, :] = appear_ref[...] * inverse_heat
    params[4:5, :] = occur_ref[...] * inverse_heat
    params[5 : 5 + steps, :] = emitted_ref[...].astype(jnp.float32)
    params[...] = jnp.transpose(params[...])

    u_copy.wait()
    for group in range(n):
        for t in range(steps):
            shift_copy(group, t).wait()

    lane_rows = lax.broadcasted_iota(jnp.int32, (LANES, length), 0)
    high_rows = lax.broadcasted_iota(jnp.int32, (high, length), 0)
    batch_unroll = math.gcd(rows, 8)
    lane_ids = lax.broadcasted_iota(jnp.int32, (rows, LANES), 1)

    def prepare(group):
        base = pl.multiple_of(group * rows, rows)
        for t in range(steps):
            gumbel[t, pl.ds(base, rows), :] = -jnp.log(-jnp.log(gumbel[t, pl.ds(base, rows), :]))

        def count(turn, carry):
            for inner in range(batch_unroll):
                row = turn * batch_unroll + inner
                ids = ids_ref[pl.ds(base + row, 1), :]
                low = jnp.bitwise_and(ids, LANES - 1)
                top = jnp.right_shift(ids, LANES.bit_length() - 1) - me * high
                low_hot = jnp.where(lane_rows == low, 1.0, 0.0).astype(jnp.bfloat16)
                top_hot = jnp.where(high_rows == top, 1.0, 0.0).astype(jnp.bfloat16)
                tally[pl.ds(pl.multiple_of(row * high, high), high), :] = lax.dot_general(
                    top_hot,
                    low_hot,
                    (((1,), (1,)), ((), ())),
                    preferred_element_type=jnp.float32,
                )
            return carry

        lax.fori_loop(0, rows // batch_unroll, count, 0)
        here = pl.ds(base, rows)
        plain, repeat, inverse_repeat, appear, occur = (
            jnp.broadcast_to(params[here, k : k + 1], (rows, LANES)) for k in range(5)
        )
        taken = [
            jnp.broadcast_to(params[here, 5 + t : 6 + t], (rows, LANES)).astype(jnp.int32)
            for t in range(steps)
        ]
        for h in range(high):
            count = tally[pl.ds(h, rows, stride=high), :]
            columns = slice(h * LANES, (h + 1) * LANES)
            for t in range(steps):
                place = pl.ds(pl.multiple_of(group * slab + t * rows, rows), rows)
                seen = count > 0
                strong[place, columns] = jnp.where(seen, repeat, plain)
                weak[place, columns] = jnp.where(seen, inverse_repeat, plain)
                charge[place, columns] = jnp.where(seen, occur * count + appear, 0.0)
                hit = lane_ids + (me * width + h * LANES) == taken[t]
                count = count + jnp.where(hit, 1.0, 0.0)

    def multiply(chunk):
        w_copy(chunk).wait()
        slot = lax.rem(chunk, SLOTS)

        def tile(i, carry):
            columns = pl.ds(pl.multiple_of(i * DOT_COLUMNS, DOT_COLUMNS), DOT_COLUMNS)
            acc[:, columns] += jnp.dot(
                xg[chunk].reshape(n * slab, depth),
                wbuf[slot, :, columns],
                preferred_element_type=jnp.float32,
            )
            return carry

        lax.fori_loop(0, width // DOT_COLUMNS, tile, 0)

        @pl.when(chunk + SLOTS < chunks)
        def _():
            w_copy(chunk + SLOTS).start()

    def turn(i, carry):
        for distance in reversed(range(1, levels)):
            chunk = i - (distance - 1)

            @pl.when(jnp.logical_and(chunk >= 0, chunk < chunks))
            def _():
                relay(chunk, distance)

        for distance in reversed(range(levels - 1)):
            chunk = i - distance

            @pl.when(
                jnp.logical_and(
                    jnp.logical_and(chunk >= 0, chunk < chunks), across_first(chunk)
                )
            )
            def _():
                relay_twin(chunk, distance)

        @pl.when(i + AHEAD < chunks)
        def _():
            start_own(i + AHEAD)

        @pl.when(i < n)
        def _():
            prepare(i)

        done = i - (levels - 1)

        @pl.when(done >= 0)
        def _():
            for level in range(levels):
                relayed = jnp.abs(z - level) < levels - 1

                @pl.when(jnp.logical_not(jnp.logical_and(across_first(done), relayed)))
                def _():
                    arrived(level * 2 + (1 - y), done)

            multiply(done)

        return carry

    lax.fori_loop(0, max(chunks + levels - 1, n), turn, 0)

    column_ids = lane_ids + me * width
    stat_lanes = lane_ids

    def scores_copy(group):
        top_row = pl.multiple_of(group * slab + (steps - 1) * rows, rows)
        return pltpu.make_async_copy(
            energies.at[pl.ds(top_row, rows), :],
            scores_hbm.at[pl.ds(pl.multiple_of(group * rows, rows), rows), :],
            out_sem.at[group],
        )

    def finish(group, carry):
        base = pl.multiple_of(group * rows, rows)
        here = pl.ds(base, rows)
        taken = [
            jnp.broadcast_to(params[here, 5 + t : 6 + t], (rows, LANES)).astype(jnp.int32)
            for t in range(steps)
        ]

        def score(i, state):
            state = list(state)
            for k in range(TAIL_COLUMNS // LANES):
                start = pl.multiple_of(i * TAIL_COLUMNS + k * LANES, LANES)
                columns = pl.ds(start, LANES)
                vocab_ids = column_ids + start
                for t in range(steps):
                    place = pl.ds(pl.multiple_of(group * slab + t * rows, rows), rows)
                    biased = acc[place, columns]
                    energy = (
                        jnp.minimum(biased * strong[place, columns], biased * weak[place, columns])
                        - charge[place, columns]
                    )
                    energies[place, columns] = energy
                    state[t] = jnp.maximum(state[t], energy)
                    state[steps + t] = jnp.maximum(
                        state[steps + t], energy + gumbel[t, here, columns]
                    )
                    state[2 * steps + t] += jnp.where(vocab_ids == taken[t], energy, 0.0)
            return tuple(state)

        lowest = jnp.full((rows, LANES), -jnp.inf, jnp.float32)
        zero = jnp.zeros((rows, LANES), jnp.float32)
        state = lax.fori_loop(
            0, width // TAIL_COLUMNS, score, (lowest,) * (2 * steps) + (zero,) * steps
        )
        scores_copy(group).start()
        tops = [jnp.max(state[t], axis=1, keepdims=True) for t in range(steps)]

        wide_tops = [jnp.broadcast_to(top, (rows, LANES)) for top in tops]

        def sums(i, state):
            state = list(state)
            for k in range(TAIL_COLUMNS // LANES):
                start = pl.multiple_of(i * TAIL_COLUMNS + k * LANES, LANES)
                for t in range(steps):
                    place = pl.ds(pl.multiple_of(group * slab + t * rows, rows), rows)
                    state[t] += jnp.exp(energies[place, pl.ds(start, LANES)] - wide_tops[t])
            return tuple(state)

        totals = lax.fori_loop(0, width // TAIL_COLUMNS, sums, (zero,) * steps)
        gathered = zero
        for t in range(steps):
            best = jnp.max(state[steps + t], axis=1, keepdims=True)
            target = jnp.sum(state[2 * steps + t], axis=1, keepdims=True)
            total = jnp.sum(totals[t], axis=1, keepdims=True)
            for k, column in enumerate((tops[t], total, best, target)):
                gathered = jnp.where(stat_lanes == k * steps + t, column, gathered)
        stats[here, :] = gathered
        return carry

    lax.fori_loop(0, n, finish, 0)

    height = exchange.shape[1]
    exchange[me] = jnp.transpose(stats[...])[:height, :]

    def trade(step):
        return pltpu.make_async_remote_copy(
            src_ref=exchange.at[me],
            dst_ref=exchange.at[me],
            send_sem=ex_send.at[step],
            recv_sem=ex_recv.at[me],
            device_id={"vocab": lax.rem(me + step, n)},
            device_id_type=MESH,
        )

    for step in range(1, n):
        trade(step).start()

    def wait_sends(chunk, carry):
        across = across_first(chunk)
        send(me, chunk, 0, twin).wait_send()
        for level in range(levels):

            @pl.when(jnp.logical_and(level != z, jnp.logical_not(across)))
            def _():
                send(level * 2 + y, chunk, 0, twin).wait_send()

            @pl.when(jnp.logical_and(level <= z, z < levels - 1))
            def _():
                send(level * 2 + y, chunk, 1, me + 2).wait_send()

                @pl.when(across)
                def _():
                    send(level * 2 + 1 - y, chunk, 1, me + 2).wait_send()

            @pl.when(jnp.logical_and(level >= z, z > 0))
            def _():
                send(level * 2 + y, chunk, 2, me - 2).wait_send()

                @pl.when(across)
                def _():
                    send(level * 2 + 1 - y, chunk, 2, me - 2).wait_send()

        return carry

    lax.fori_loop(0, chunks, wait_sends, 0)

    for step in range(1, n):
        other = lax.rem(me + step, n)
        pltpu.make_async_remote_copy(
            src_ref=exchange.at[other],
            dst_ref=exchange.at[other],
            send_sem=ex_send.at[step],
            recv_sem=ex_recv.at[other],
            device_id={"vocab": other},
            device_id_type=MESH,
        ).wait_recv()
    for step in range(1, n):
        trade(step).wait_send()

    every = exchange[...]
    tops = every[:, 0:steps, :]
    top = jnp.max(tops, axis=0)
    total = jnp.sum(every[:, steps : 2 * steps, :] * jnp.exp(tops - top[None]), axis=0)
    normalizer = top + jnp.log(total)
    stats_out[0:steps, :] = jnp.max(every[:, 2 * steps : 3 * steps, :], axis=0)
    stats_out[steps : 2 * steps, :] = (
        jnp.sum(every[:, 3 * steps : 4 * steps, :], axis=0) - normalizer
    )
    stats_out[2 * steps : 3 * steps, :] = normalizer
    for group in range(n):
        scores_copy(jnp.int32(group)).wait()


def fused_device(n, chunks, *args):
    (x, w, shift, u, ids, emitted, heat, repeat, appear, occur) = args
    steps, rows, model = x.shape
    batch, width = shift.shape
    depth = model // chunks
    high = width // LANES
    height = -(-4 * steps // 8) * 8
    anywhere = pl.BlockSpec(memory_space=pl.ANY)
    inside = pl.BlockSpec(memory_space=pltpu.VMEM)
    dma = pltpu.SemaphoreType.DMA
    scores, stats = pl.pallas_call(
        functools.partial(fused_kernel, n, chunks),
        out_shape=(
            jax.ShapeDtypeStruct((batch, width), jnp.float32),
            jax.ShapeDtypeStruct((3 * steps, batch), jnp.float32),
        ),
        in_specs=[anywhere] * 4 + [inside] * 6,
        out_specs=(anywhere, inside),
        scratch_shapes=[
            pltpu.VMEM((chunks, n, steps * rows, depth), x.dtype),
            pltpu.VMEM((SLOTS, depth, width), w.dtype),
            pltpu.VMEM((steps * batch, width), jnp.float32),
            pltpu.VMEM((steps, batch, width), jnp.float32),
            pltpu.VMEM((steps * batch, width), jnp.float32),
            pltpu.VMEM((steps * batch, width), jnp.float32),
            pltpu.VMEM((steps * batch, width), jnp.float32),
            pltpu.VMEM((rows * high, LANES), jnp.float32),
            pltpu.VMEM((steps * batch, width), jnp.float32),
            pltpu.VMEM((LANES, LANES), jnp.float32),
            pltpu.VMEM((batch, LANES), jnp.float32),
            pltpu.VMEM((n, height, batch), jnp.float32),
            dma((chunks, steps)),
            dma((SLOTS,)),
            dma((1 + n * steps,)),
            dma((n,)),
            dma((chunks, n, 3)),
            dma((chunks, n)),
            dma((n,)),
            dma((n,)),
        ],
        compiler_params=pltpu.CompilerParams(
            collective_id=0, has_side_effects=True, vmem_limit_bytes=60 * 1024 * 1024
        ),
    )(
        x,
        w,
        shift,
        u,
        ids,
        jnp.transpose(emitted),
        heat[None],
        repeat[None],
        appear[None],
        occur[None],
    )
    best = stats[:steps]
    target_logprob = stats[steps : 2 * steps]
    return best, target_logprob, scores - stats[3 * steps - 1][:, None]


def per_device_any(n, *args):
    x, w, shift = args[:3]
    steps, rows, model = x.shape
    batch, width = shift.shape
    chunks = 12
    fits = (
        n % 2 == 0
        and n > 2
        and rows % 16 == 0
        and batch == LANES
        and rows * n == batch
        and width % max(DOT_COLUMNS, TAIL_COLUMNS) == 0
        and (width // LANES) % 8 == 0
        and model % (chunks * LANES) == 0
        and args[4].shape[1] % LANES == 0
        and 4 * steps <= LANES
    )
    if fits:
        return fused_device(n, chunks, *args)
    return per_device(*args)


def solution(mesh):
    in_specs = (
        P(None, ("batch", "vocab"), None),
        P(None, "vocab"),
        P("batch", "vocab"),
        P(None, "batch", "vocab"),
        P("batch", None),
        P("batch", None),
        P("batch"),
        P("batch"),
        P("batch"),
        P("batch"),
    )
    out_specs = (P(None, "batch"), P(None, "batch"), P("batch", "vocab"))
    return jax.shard_map(
        functools.partial(per_device_any, mesh.shape["vocab"]),
        mesh=mesh, in_specs=in_specs, out_specs=out_specs, check_vma=False
    )
```
